512 devices in a mesh: row: 32 (over z_lo, x), col: 16 (over z_hi, y, core).
Axes of the slice: x: 4, y: 4, z: 16 (z_hi: 2, z_lo: 8; z = z_hi * 8 + z_lo), core: 2. Of those that a mesh axis runs over, the one named last changes fastest.
Arguments:
- weight: float32 [16384, 16384], P('row', 'col'), may hold values from -6 to 6
- blocks: float32 [5, 16384, 512], P(None, ('row', 'col')), may hold values from -0.2 to 1.2
Outputs:
- merged: float32 [16384, 16384], P('row', 'col')
The draws below stay inside these ranges and needn't reach their ends.
All inputs are finite; a program needn't handle non-finite values.
Results may differ from the reference program's by a relative error of at most 0.00017.
Values sent between devices are 32-bit elements; how exact they have to be, the bound alone decides.
A program may use at most 64 MiB of HBM per device.

```python
import math
import jax
import jax.numpy as jnp
from jax import lax

BS = 512
HALF = 256
COLS_DEV = 1024
FACTORS = 5
ROWS = 16384
COLUMNS = 16384
N_ROW = 32
N_COL = 16


def draw_blocks(key, part):
    row_index = jnp.arange(ROWS)
    identity = (jnp.arange(BS)[None, :] == (row_index % HALF)[:, None]).astype(jnp.float32)
    random_part = jnp.clip(jax.random.normal(key, (FACTORS, ROWS, BS), jnp.float32), -6.0, 6.0)
    scaled = jnp.clip(random_part * (0.5 / math.sqrt(BS)), -0.2, 0.2)
    return identity[None] + scaled


def block_levels(own_key, extent, pieces, smallest, high):
    level, own = 1.0, jax.random.fold_in(own_key, 6)
    for dim, parts in pieces:
        heights = jnp.exp(jax.random.uniform(jax.random.fold_in(own, dim), (parts,), jnp.float32, smallest / len(pieces), high / len(pieces)))
        level = level * jnp.repeat(heights, extent[dim] // parts).reshape([-1 if axis == dim else 1 for axis in range(len(extent))])
    return level


def noise(stream_key, extent, deviation, reach, shards=(), held_as=jnp.bfloat16):
    gain = block_levels(stream_key, extent, shards, -0.22, 0.18) if shards else 1.0
    drawn = jax.random.normal(stream_key, extent, jnp.float32) * deviation * gain
    return jnp.minimum(jnp.maximum(drawn, -reach), reach).astype(held_as)


def setup_inputs(seed: int = 0) -> dict:
    key_of = jax.random.split(jax.random.key(seed), 3)
    weight = noise(key_of[0], (ROWS, COLUMNS), 1.0, 6.0, ((0, 32), (1, 16)), jnp.float32)
    blocks = draw_blocks(jax.random.fold_in(key_of[2], 71), 0)
    return {"weight": weight, "blocks": blocks}


def reference(weight, blocks):
    bit_count = N_ROW.bit_length() - 1
    column_blocks = weight.reshape(ROWS, N_COL, COLS_DEV).transpose(1, 0, 2)

    def apply_factors(weight_slab):
        for factor in range(FACTORS):
            distance_bit = factor % bit_count
            grouped = weight_slab.reshape(N_ROW // (2 * 2 ** distance_bit), 2, 2 ** distance_bit, 2, HALF, COLS_DEV)
            partner = jnp.flip(grouped, axis=1).reshape(N_ROW, 2, HALF, COLS_DEV)
            resident = weight_slab.reshape(N_ROW, 2, HALF, COLS_DEV)
            coefficients = blocks[factor].reshape(N_ROW, 2, HALF, BS)
            stacked = jnp.concatenate([resident, partner], axis=2)
            updated = jnp.einsum("athj,atjc->athc", coefficients, stacked, precision=lax.Precision.HIGHEST)
            weight_slab = updated.reshape(ROWS, COLS_DEV)
        return weight_slab

    result = lax.map(apply_factors, column_blocks)
    return result.transpose(1, 0, 2).reshape(ROWS, N_COL * COLS_DEV)
```

```python
import functools

import jax
import jax.numpy as jnp
from jax import lax
from jax.experimental import pallas as pl
from jax.experimental.pallas import tpu as pltpu
from jax.sharding import PartitionSpec as P

MESH = pl.DeviceIdType.MESH
FACTORS = 5
UNITS = 16
HALF = 256
LANES = 128
GROUP = 8
LAGS = (2, 4, 6, 8, 10)


def partner_of(index, stride):
    return index + stride - 2 * stride * lax.rem(index // stride, 2)


def remote(src, dst, send, recv, where):
    return pltpu.make_async_remote_copy(
        src_ref=src, dst_ref=dst, send_sem=send, recv_sem=recv, device_id=where, device_id_type=MESH
    )


def kernel(
    weight, blocks, out, w, r, done, raw, coef,
    load_sem, store_sem, send_sem, recv_sem, own_sem, gather_send, gather_recv, swap_send, swap_recv,
):
    row, col = lax.axis_index("row"), lax.axis_index("col")
    z_hi, slot = col // GROUP, lax.rem(col, GROUP)
    mates = [z_hi * GROUP + lax.rem(slot + i, GROUP) for i in range(1, GROUP)]
    across = lax.rem(col + GROUP, 2 * GROUP)
    partners = [partner_of(row, 1 << k) for k in range(FACTORS)]

    def half_of(u):
        return lax.rem(u // (UNITS // 2) + z_hi, 2)

    def tile(ref, u):
        rows = pl.ds(pl.multiple_of(half_of(u) * HALF, HALF), HALF)
        columns = pl.ds(pl.multiple_of(lax.rem(u, UNITS // 2) * LANES, LANES), LANES)
        return ref.at[rows, columns]

    def load(u):
        return pltpu.make_async_copy(tile(weight, u), w.at[0, u], load_sem.at[u])

    def store(u):
        return pltpu.make_async_copy(done.at[u], tile(out, u), store_sem.at[u])

    def exchange(k, u):
        return remote(w.at[k, u], r.at[k, u], send_sem.at[k, u], recv_sem.at[k, u], {"row": partners[k]})

    def own_copy(k):
        return pltpu.make_async_copy(blocks.at[k], raw.at[k, z_hi, slot], own_sem.at[k])

    def swap(k):
        return remote(blocks.at[k], raw.at[k, z_hi, slot], swap_send.at[k], swap_recv.at[k], {"col": across})

    def swapped(k):
        return raw.at[k, 1 - z_hi, slot]

    def gather(k, half, src, mate):
        return remote(
            src, raw.at[k, half, slot], gather_send.at[k, half], gather_recv.at[k, half], {"col": mate}
        )

    def gathered(k, half):
        part = raw.at[k, half, pl.ds(0, GROUP - 1)]
        return remote(part, part, gather_send.at[k, half], gather_recv.at[k, half], {"col": mates[0]})

    @pl.loop(0, UNITS)
    def _(u):
        load(u).start()

    for k in range(FACTORS):
        own_copy(k).start()

    barrier = pltpu.get_barrier_semaphore()
    for p in partners:
        pl.semaphore_signal(barrier, inc=1, device_id={"row": p}, device_id_type=MESH)
    for m in mates + [across]:
        pl.semaphore_signal(barrier, inc=1, device_id={"col": m}, device_id_type=MESH)
    pl.semaphore_wait(barrier, FACTORS + GROUP)

    for k in range(FACTORS):
        for m in mates:
            gather(k, z_hi, blocks.at[k], m).start()
        swap(k).start()

    def prepare(k, half):
        gathered(k, half).wait_recv()
        block = raw[k, half].reshape(HALF, 2 * HALF)
        high = block.astype(jnp.bfloat16)
        coef[k, half, pl.ds(0, HALF), :] = high
        coef[k, half, pl.ds(HALF, HALF), :] = (block - high.astype(jnp.float32)).astype(jnp.bfloat16)

    def advance(k, u):
        half = half_of(u)

        @pl.when(u == 0)
        def _():
            own_copy(k).wait()

        @pl.when(lax.rem(u, UNITS // 2) == 0)
        def _():
            prepare(k, half)

        exchange(k, u).wait_recv()
        x = jnp.concatenate([w[k, u], r[k, u]], axis=0)
        high = x.astype(jnp.bfloat16)
        low = (x - high.astype(jnp.float32)).astype(jnp.bfloat16)
        product = jnp.dot(
            coef[k, half], jnp.concatenate([high, low], axis=1), preferred_element_type=jnp.float32
        )
        y = (product[:HALF, :LANES] + (product[:HALF, LANES:] + product[HALF:, :LANES])) + product[HALF:, LANES:]
        if k + 1 < FACTORS:
            w[k + 1, u] = y
            exchange(k + 1, u).start()
        else:
            done[u] = y
            store(u).start()

    @pl.loop(0, UNITS + LAGS[-1])
    def _(step):
        @pl.when(step < UNITS)
        def _():
            load(step).wait()
            exchange(0, step).start()

        for k in reversed(range(FACTORS)):
            u = step - LAGS[k]

            @pl.when((u >= 0) & (u < UNITS))
            def _():
                advance(k, u)

        @pl.when((step >= 5) & (step < 5 + FACTORS))
        def _():
            k = step - 5
            swap(k).wait_recv()
            for m in mates:
                gather(k, 1 - z_hi, swapped(k), m).start()

    @pl.loop(0, UNITS)
    def _(u):
        store(u).wait()
        for k in range(FACTORS):
            exchange(k, u).wait_send()

    for k in range(FACTORS):
        swap(k).wait_send()
        for half in range(2):
            gathered(k, half).wait_send()


def body(weight, blocks):
    f32 = jnp.float32
    dma = pltpu.SemaphoreType.DMA
    tiles = (UNITS, HALF, LANES)
    return pl.pallas_call(
        kernel,
        out_shape=jax.ShapeDtypeStruct(weight.shape, weight.dtype),
        in_specs=[pl.BlockSpec(memory_space=pl.ANY)] * 2,
        out_specs=pl.BlockSpec(memory_space=pl.ANY),
        scratch_shapes=[
            pltpu.VMEM((FACTORS,) + tiles, f32),
            pltpu.VMEM((FACTORS,) + tiles, f32),
            pltpu.VMEM(tiles, f32),
            pltpu.VMEM((FACTORS, 2, GROUP, HALF // GROUP, 2 * HALF), f32),
            pltpu.VMEM((FACTORS, 2, 2 * HALF, 2 * HALF), jnp.bfloat16),
            dma((UNITS,)),
            dma((UNITS,)),
            dma((FACTORS, UNITS)),
            dma((FACTORS, UNITS)),
            dma((FACTORS,)),
            dma((FACTORS, 2)),
            dma((FACTORS, 2)),
            dma((FACTORS,)),
            dma((FACTORS,)),
        ],
        compiler_params=pltpu.CompilerParams(
            collective_id=0, has_side_effects=True, vmem_limit_bytes=60 * 1024 * 1024
        ),
    )(weight, blocks)


def solution(mesh):
    return jax.shard_map(
        body,
        mesh=mesh,
        in_specs=(P("row", "col"), P(None, ("row", "col"), None)),
        out_specs=P("row", "col"),
        check_vma=False,
    )
```

```python
import functools

import jax
import jax.numpy as jnp
from jax import lax
from jax.experimental import pallas as pl
from jax.experimental.pallas import tpu as pltpu
from jax.sharding import PartitionSpec as P

MESH = pl.DeviceIdType.MESH
FACTORS = 5
UNITS = 16
HALF = 256
LANES = 128
GROUP = 8
SETS = 7
LENT = ((5, 3), (6, 4))
AHEAD = 2
LAGS = (0, 2, 4, 6, 8)
SWAP_STEP = 3


def partner_of(index, stride):
    return index + stride - 2 * stride * lax.rem(index // stride, 2)


def remote(src, dst, send, recv, where):
    return pltpu.make_async_remote_copy(
        src_ref=src, dst_ref=dst, send_sem=send, recv_sem=recv, device_id=where, device_id_type=MESH
    )


def kernel(
    weight, blocks, out, w, r, done, w_lent, r_lent, raw, coef,
    load_sem, store_sem, send_sem, recv_sem, lent_send, lent_recv, back_send, back_recv, slab_send, slab_recv, own_sem, gather_send, gather_recv, swap_send, swap_recv,
):
    row, col = lax.axis_index("row"), lax.axis_index("col")
    z_hi, slot = col // GROUP, lax.rem(col, GROUP)
    mates = [z_hi * GROUP + lax.rem(slot + i, GROUP) for i in range(1, GROUP)]
    across = lax.rem(col + GROUP, 2 * GROUP)
    partners = [partner_of(row, 1 << k) for k in range(FACTORS)]
    x, z_lo = lax.rem(row, 4), row // 4
    lender = (z_lo == 1) | (z_lo == 6)
    host = (z_lo == 3) | (z_lo == 4)
    facing_lent = (z_lo == 2) | (z_lo == 5)
    pair = partners[3]
    lent_far = partner_of(pair, 16)
    far_host = partner_of(partners[4], 8)

    def half_of(u):
        return lax.rem(u // (UNITS // 2) + z_hi, 2)

    def tile(ref, u):
        rows = pl.ds(pl.multiple_of(half_of(u) * HALF, HALF), HALF)
        columns = pl.ds(pl.multiple_of(lax.rem(u, UNITS // 2) * LANES, LANES), LANES)
        return ref.at[rows, columns]

    def load(u):
        return pltpu.make_async_copy(tile(weight, u), w.at[0, u], load_sem.at[u])

    def store(u):
        return pltpu.make_async_copy(done.at[u], tile(out, u), store_sem.at[u])

    def exchange(k, u):
        return remote(w.at[k, u], r.at[k, u], send_sem.at[k, u], recv_sem.at[k, u], {"row": partners[k]})

    def to_lent(u):
        return remote(w.at[4, u], r_lent.at[u], send_sem.at[4, u], lent_recv.at[u], {"row": far_host})

    def from_lent(u):
        return remote(w_lent.at[u], r.at[4, u], lent_send.at[u], recv_sem.at[4, u], {"row": lent_far})

    def give_back(u):
        return remote(r_lent.at[u], done.at[u], back_send.at[u], back_recv.at[u], {"row": pair})

    def slab(i, column, which):
        k, source = LENT[i]
        return remote(
            blocks.at[source], raw.at[k, z_hi, slot], slab_send.at[i, which], slab_recv.at[i, z_hi],
            {"row": pair, "col": column},
        )

    def slab_wait(i, half):
        part = raw.at[LENT[i][0], half, slot]
        remote(part, part, slab_send.at[i, 0], slab_recv.at[i, half], {"row": pair, "col": across}).wait_recv()

    def own_copy(k):
        return pltpu.make_async_copy(blocks.at[k], raw.at[k, z_hi, slot], own_sem.at[k])

    def swap(k):
        return remote(blocks.at[k], raw.at[k, z_hi, slot], swap_send.at[k], swap_recv.at[k], {"col": across})

    def swapped(k):
        return raw.at[k, 1 - z_hi, slot]

    def gather(k, half, src, mate):
        return remote(
            src, raw.at[k, half, slot], gather_send.at[k, half], gather_recv.at[k, half], {"col": mate}
        )

    def gathered(k, half):
        part = raw.at[k, half, pl.ds(0, GROUP - 1)]
        return remote(part, part, gather_send.at[k, half], gather_recv.at[k, half], {"col": mates[0]})

    @pl.loop(0, UNITS)
    def _(u):
        load(u).start()

    for k in range(FACTORS):
        own_copy(k).start()

    barrier = pltpu.get_barrier_semaphore()

    def greet(where):
        pl.semaphore_signal(barrier, inc=1, device_id=where, device_id_type=MESH)

    for p in partners[:4]:
        greet({"row": p})
    for m in mates + [across]:
        greet({"col": m})

    @pl.when(lender)
    def _():
        greet({"row": pair, "col": across})

    @pl.when(facing_lent)
    def _():
        greet({"row": far_host})

    @pl.when(host)
    def _():
        greet({"row": pair, "col": across})
        greet({"row": lent_far})

    @pl.when(jnp.logical_not(lender | facing_lent))
    def _():
        greet({"row": partners[4]})

    @pl.when(host)
    def _():
        pl.semaphore_wait(barrier, FACTORS + GROUP + 2)

    @pl.when(jnp.logical_not(host))
    def _():
        pl.semaphore_wait(barrier, FACTORS + GROUP)

    for u in range(AHEAD):
        load(u).wait()
        exchange(0, u).start()

    @pl.when(lender)
    def _():
        for i in range(2):
            slab(i, col, 0).start()

    def spread(k):
        for m in mates:
            gather(k, z_hi, blocks.at[k], m).start()

    def spread_lent(i):
        @pl.when(host)
        def _():
            slab_wait(i, z_hi)
            for m in mates:
                gather(LENT[i][0], z_hi, raw.at[LENT[i][0], z_hi, slot], m).start()

    for k in range(4):
        spread(k)
    spread_lent(0)
    spread(4)
    spread_lent(1)
    for k in range(FACTORS):
        swap(k).start()

    @pl.when(lender)
    def _():
        for i in range(2):
            slab(i, across, 1).start()

    def prepare(k, half):
        gathered(k, half).wait_recv()
        block = raw[k, half].reshape(HALF, 2 * HALF)
        high = block.astype(jnp.bfloat16)
        coef[k, half, pl.ds(0, HALF), :] = high
        coef[k, half, pl.ds(HALF, HALF), :] = (block - high.astype(jnp.float32)).astype(jnp.bfloat16)

    def multiply(k, half, own, other):
        x = jnp.concatenate([own, other], axis=0)
        high = x.astype(jnp.bfloat16)
        low = (x - high.astype(jnp.float32)).astype(jnp.bfloat16)
        product = jnp.dot(
            coef[k, half], jnp.concatenate([high, low], axis=1), preferred_element_type=jnp.float32
        )
        cross = product[:HALF, LANES:] + product[HALF:, :LANES]
        return (product[:HALF, :LANES] + cross) + product[HALF:, LANES:]

    def advance(k, u):
        half = half_of(u)

        @pl.when(u == 0)
        def _():
            own_copy(k).wait()

        @pl.when(lax.rem(u, UNITS // 2) == 0)
        def _():
            prepare(k, half)

        exchange(k, u).wait_recv()
        y = multiply(k, half, w[k, u], r[k, u])
        if k + 1 == FACTORS:
            done[u] = y
            store(u).start()
        else:
            w[k + 1, u] = y
            if k < 2:
                exchange(k + 1, u).start()
            elif k == 2:
                pl.when(jnp.logical_not(host))(lambda: exchange(3, u).start())
            else:
                pl.when(facing_lent)(lambda: to_lent(u).start())
                pl.when(jnp.logical_not(facing_lent))(lambda: exchange(4, u).start())

    def advance_lent(i, u):
        half = half_of(u)
        k, source = LENT[i]

        @pl.when(lax.rem(u, UNITS // 2) == 0)
        def _():
            prepare(k, half)

        if i == 0:
            w_lent[u] = multiply(k, half, r[3, u], w[3, u])
            from_lent(u).start()
        else:
            to_lent(u).wait_recv()
            r_lent[u] = multiply(k, half, w_lent[u], r_lent[u])
            give_back(u).start()

    @pl.loop(0, UNITS + LAGS[-1])
    def _(step):
        @pl.when(step + AHEAD < UNITS)
        def _():
            load(step + AHEAD).wait()
            exchange(0, step + AHEAD).start()

        for k in reversed(range(FACTORS)):
            u = step - LAGS[k]
            here = (u >= 0) & (u < UNITS)
            if k > 2:
                here = here & jnp.logical_not(lender)

            @pl.when(here)
            def _():
                advance(k, u)
                if k > 2:
                    pl.when(host)(lambda: advance_lent(k - 3, u))

        @pl.when((step >= SWAP_STEP) & (step < SWAP_STEP + FACTORS))
        def _():
            k = step - SWAP_STEP
            swap(k).wait_recv()
            for m in mates:
                gather(k, 1 - z_hi, swapped(k), m).start()

        for i in range(2):
            @pl.when(host & (step == SWAP_STEP + 4 + i))
            def _():
                k = LENT[i][0]
                slab_wait(i, 1 - z_hi)
                for m in mates:
                    gather(k, 1 - z_hi, swapped(k), m).start()

    @pl.when(lender)
    def _():
        for k in range(3, FACTORS):
            own_copy(k).wait()
            for half in range(2):
                gathered(k, half).wait_recv()

        @pl.loop(0, UNITS)
        def _(u):
            give_back(u).wait_recv()
            store(u).start()

    @pl.loop(0, UNITS)
    def _(u):
        store(u).wait()
        for k in range(3):
            exchange(k, u).wait_send()

        @pl.when(jnp.logical_not(host))
        def _():
            exchange(3, u).wait_send()

        @pl.when(jnp.logical_not(lender))
        def _():
            exchange(4, u).wait_send()

        @pl.when(host)
        def _():
            from_lent(u).wait_send()
            give_back(u).wait_send()

    for k in range(FACTORS):
        swap(k).wait_send()
        for half in range(2):
            gathered(k, half).wait_send()

    for i in range(2):
        @pl.when(host)
        def _():
            for half in range(2):
                gathered(LENT[i][0], half).wait_send()

        @pl.when(lender)
        def _():
            slab(i, col, 0).wait_send()
            slab(i, across, 1).wait_send()


def body(weight, blocks):
    f32 = jnp.float32
    dma = pltpu.SemaphoreType.DMA
    tiles = (UNITS, HALF, LANES)
    return pl.pallas_call(
        kernel,
        out_shape=jax.ShapeDtypeStruct(weight.shape, weight.dtype),
        in_specs=[pl.BlockSpec(memory_space=pl.ANY)] * 2,
        out_specs=pl.BlockSpec(memory_space=pl.ANY),
        scratch_shapes=[
            pltpu.VMEM((FACTORS,) + tiles, f32),
            pltpu.VMEM((FACTORS,) + tiles, f32),
            pltpu.VMEM(tiles, f32),
            pltpu.VMEM(tiles, f32),
            pltpu.VMEM(tiles, f32),
            pltpu.VMEM((SETS, 2, GROUP, HALF // GROUP, 2 * HALF), f32),
            pltpu.VMEM((SETS, 2, 2 * HALF, 2 * HALF), jnp.bfloat16),
            dma((UNITS,)),
            dma((UNITS,)),
            dma((FACTORS, UNITS)),
            dma((FACTORS, UNITS)),
            dma((UNITS,)),
            dma((UNITS,)),
            dma((UNITS,)),
            dma((UNITS,)),
            dma((2, 2)),
            dma((2, 2)),
            dma((FACTORS,)),
            dma((SETS, 2)),
            dma((SETS, 2)),
            dma((FACTORS,)),
            dma((FACTORS,)),
        ],
        compiler_params=pltpu.CompilerParams(
            collective_id=0, has_side_effects=True, vmem_limit_bytes=60 * 1024 * 1024
        ),
    )(weight, blocks)


def solution(mesh):
    return jax.shard_map(
        body,
        mesh=mesh,
        in_specs=(P("row", "col"), P(None, ("row", "col"), None)),
        out_specs=P("row", "col"),
        check_vma=False,
    )
```

```python
import functools

import jax
import jax.numpy as jnp
from jax import lax
from jax.experimental import pallas as pl
from jax.experimental.pallas import tpu as pltpu
from jax.sharding import PartitionSpec as P

MESH = pl.DeviceIdType.MESH
FACTORS = 5
UNITS = 16
HALF = 256
LANES = 128
GROUP = 8
SETS = 7
LENT = ((5, 3), (6, 4))
FIRST = (0, 2, 6, 10, 13)
PERIOD = (2, 2, 2, 2, 2)
STEPS = FIRST[-1] + PERIOD[-1] * (UNITS - 1) + 1
SWAP_STEP = 7


def partner_of(index, stride):
    return index + stride - 2 * stride * lax.rem(index // stride, 2)


def remote(src, dst, send, recv, where):
    return pltpu.make_async_remote_copy(
        src_ref=src, dst_ref=dst, send_sem=send, recv_sem=recv, device_id=where, device_id_type=MESH
    )


def kernel(
    weight, blocks, out, w, r, done, w_lent, r_lent, raw, coef,
    load_sem, store_sem, send_sem, recv_sem, lent_send, lent_recv, back_send, back_recv, slab_send, slab_recv, own_sem, fan_send, fan_recv, swap_send, swap_recv,
):
    row, col = lax.axis_index("row"), lax.axis_index("col")
    z_hi, slot = col // GROUP, lax.rem(col, GROUP)
    y, core = slot // 2, lax.rem(slot, 2)
    turn = 1 - 2 * core
    front = lax.rem(y + 4 + turn, 4) * 2 + core
    back = lax.rem(y + 4 - turn, 4) * 2 + core
    far = lax.rem(y + 2, 4) * 2 + core
    twin = y * 2 + 1 - core
    own, other = z_hi, 1 - z_hi
    across = lax.rem(col + GROUP, 2 * GROUP)
    partners = [partner_of(row, 1 << k) for k in range(FACTORS)]
    x, z_lo = lax.rem(row, 4), row // 4
    lender = (z_lo == 1) | (z_lo == 6)
    host = (z_lo == 3) | (z_lo == 4)
    facing_lent = (z_lo == 2) | (z_lo == 5)
    pair = partners[3]
    lent_far = partner_of(pair, 16)
    far_host = partner_of(partners[4], 8)

    def half_of(u):
        return lax.rem(u // (UNITS // 2) + z_hi, 2)

    def tile(ref, u):
        rows = pl.ds(pl.multiple_of(half_of(u) * HALF, HALF), HALF)
        columns = pl.ds(pl.multiple_of(lax.rem(u, UNITS // 2) * LANES, LANES), LANES)
        return ref.at[rows, columns]

    def load(u):
        return pltpu.make_async_copy(tile(weight, u), w.at[0, u], load_sem.at[u])

    def store(u):
        return pltpu.make_async_copy(done.at[u], tile(out, u), store_sem.at[u])

    def exchange(k, u):
        return remote(w.at[k, u], r.at[k, u], send_sem.at[k, u], recv_sem.at[k, u], {"row": partners[k]})

    def to_lent(u):
        return remote(w.at[4, u], r_lent.at[u], send_sem.at[4, u], lent_recv.at[u], {"row": far_host})

    def from_lent(u):
        return remote(w_lent.at[u], r.at[4, u], lent_send.at[u], recv_sem.at[4, u], {"row": lent_far})

    def give_back(u):
        return remote(r_lent.at[u], done.at[u], back_send.at[u], back_recv.at[u], {"row": pair})

    def slab(i, column, which):
        k, source = LENT[i]
        return remote(
            blocks.at[source], raw.at[k, z_hi, slot], slab_send.at[i, which], slab_recv.at[i, z_hi],
            {"row": pair, "col": column},
        )

    def slab_wait(i, half):
        part = raw.at[LENT[i][0], half, slot]
        remote(part, part, slab_send.at[i, 0], slab_recv.at[i, half], {"row": pair, "col": across}).wait_recv()

    def own_copy(k):
        return pltpu.make_async_copy(blocks.at[k], raw.at[k, z_hi, slot], own_sem.at[k])

    def swap(k):
        return remote(blocks.at[k], raw.at[k, z_hi, slot], swap_send.at[k], swap_recv.at[k], {"col": across})

    def fan(k, half, source, to):
        return remote(
            raw.at[k, half, source], raw.at[k, half, source], fan_send.at[k, half], fan_recv.at[k, half, source],
            {"col": z_hi * GROUP + to},
        )

    def fan_start(k, half):
        for to in (front, back, twin):
            fan(k, half, slot, to).start()

    def fan_relay(k, half):
        fan(k, half, back, front).wait_recv()
        fan(k, half, back, front).start()
        fan(k, half, back, twin).start()

    def fan_rest(k, half):
        for source in (front, far):
            fan(k, half, source, twin).wait_recv()
            fan(k, half, source, twin).start()

    def fan_collect(k, half):
        for i in range(4):
            fan(k, half, 2 * i + 1 - core, twin).wait_recv()

    def fan_drain(k, half):
        part = raw.at[k, half, pl.ds(0, GROUP - 1)]
        remote(part, part, fan_send.at[k, half], fan_recv.at[k, half, 0], {"col": across}).wait_send()

    @pl.loop(0, UNITS)
    def _(u):
        load(u).start()

    for k in range(FACTORS):
        own_copy(k).start()

    barrier = pltpu.get_barrier_semaphore()

    def greet(where):
        pl.semaphore_signal(barrier, inc=1, device_id=where, device_id_type=MESH)

    for p in partners[:4]:
        greet({"row": p})
    for mate in (front, back, twin):
        greet({"col": z_hi * GROUP + mate})
    greet({"col": across})

    @pl.when(lender)
    def _():
        greet({"row": pair, "col": across})

    @pl.when(facing_lent)
    def _():
        greet({"row": far_host})

    @pl.when(host)
    def _():
        greet({"row": pair, "col": across})
        greet({"row": lent_far})

    @pl.when(jnp.logical_not(lender | facing_lent))
    def _():
        greet({"row": partners[4]})

    @pl.when(host)
    def _():
        pl.semaphore_wait(barrier, FACTORS + 4 + 2)

    @pl.when(jnp.logical_not(host))
    def _():
        pl.semaphore_wait(barrier, FACTORS + 4)

    for u in range(2):
        load(u).wait()
        exchange(0, u).start()

    @pl.when(lender)
    def _():
        for i in range(2):
            slab(i, col, 0).start()

    keeper = jnp.logical_not(lender)

    def on(condition, *tasks):
        def run():
            @pl.when(condition)
            def _():
                for f, *args in tasks:
                    f(*args)
        return run

    def always(*tasks):
        def run():
            for f, *args in tasks:
                f(*args)
        return run

    def first(k):
        own_copy(k).wait()
        fan_start(k, own)

    def take_swap(k):
        swap(k).wait_recv()
        fan_start(k, other)

    def take_slab(i, half):
        slab_wait(i, half)
        fan_start(LENT[i][0], half)

    for k in range(3):
        first(k)
    on(keeper, (first, 3), (first, 4))()
    for k in range(3):
        swap(k).start()
    on(keeper, (lambda: [swap(k).start() for k in (3, 4)],))()

    @pl.when(lender)
    def _():
        for i in range(2):
            slab(i, across, 1).start()

    for k in range(2):
        fan_relay(k, own)
    fan_rest(0, own)
    on(host, (take_slab, 0, own), (take_slab, 1, own))()

    plan = {}

    def at(step, task):
        plan.setdefault(step, []).append(task)

    at(0, always((fan_rest, 1, own), (fan_relay, 2, own)))
    at(1, always((fan_rest, 2, own)))
    at(1, on(keeper, (fan_relay, 3, own)))
    at(1, on(host, (fan_relay, 5, own)))
    at(2, on(keeper, (fan_rest, 3, own), (fan_relay, 4, own)))
    at(2, on(host, (fan_rest, 5, own), (fan_relay, 6, own)))
    at(3, on(keeper, (fan_rest, 4, own)))
    at(3, on(host, (fan_rest, 6, own)))
    for place, k in enumerate((0, 1, 2, 3, 5, 4, 6)):
        take = (take_swap, k) if k < FACTORS else (take_slab, k - FACTORS, other)
        who = always if k < 3 else functools.partial(on, keeper if k < FACTORS else host)
        at(SWAP_STEP + 2 * place, who(take))
        at(SWAP_STEP + 2 * place + 1, who((fan_relay, k, other)))
        at(SWAP_STEP + 2 * place + 2, who((fan_rest, k, other)))

    def prepare(k, half):
        fan_collect(k, half)
        block = raw[k, half].reshape(HALF, 2 * HALF)
        high = block.astype(jnp.bfloat16)
        coef[k, half, pl.ds(0, HALF), :] = high
        coef[k, half, pl.ds(HALF, HALF), :] = (block - high.astype(jnp.float32)).astype(jnp.bfloat16)

    def multiply(k, half, own, other):
        x = jnp.concatenate([own, other], axis=0)
        high = x.astype(jnp.bfloat16)
        low = (x - high.astype(jnp.float32)).astype(jnp.bfloat16)
        product = jnp.dot(
            coef[k, half], jnp.concatenate([high, low], axis=1), preferred_element_type=jnp.float32
        )
        cross = product[:HALF, LANES:] + product[HALF:, :LANES]
        return (product[:HALF, :LANES] + cross) + product[HALF:, LANES:]

    def advance(k, u):
        half = half_of(u)

        @pl.when(lax.rem(u, UNITS // 2) == 0)
        def _():
            prepare(k, half)

        exchange(k, u).wait_recv()
        y = multiply(k, half, w[k, u], r[k, u])
        if k + 1 == FACTORS:
            done[u] = y
            store(u).start()
        else:
            w[k + 1, u] = y
            if k < 2:
                exchange(k + 1, u).start()
            elif k == 2:
                pl.when(jnp.logical_not(host))(lambda: exchange(3, u).start())
            else:
                pl.when(facing_lent)(lambda: to_lent(u).start())
                pl.when(jnp.logical_not(facing_lent))(lambda: exchange(4, u).start())

    def advance_lent(i, u):
        half = half_of(u)
        k, source = LENT[i]

        @pl.when(lax.rem(u, UNITS // 2) == 0)
        def _():
            prepare(k, half)

        if i == 0:
            w_lent[u] = multiply(k, half, r[3, u], w[3, u])
            from_lent(u).start()
        else:
            to_lent(u).wait_recv()
            r_lent[u] = multiply(k, half, w_lent[u], r_lent[u])
            give_back(u).start()

    @pl.loop(0, STEPS)
    def _(step):
        for k in reversed(range(FACTORS)):
            since = step - FIRST[k]
            u = since // PERIOD[k]
            here = (since >= 0) & (lax.rem(since, PERIOD[k]) == 0) & (u < UNITS)
            if k > 2:
                here = here & keeper

            @pl.when(here)
            def _():
                advance(k, u)
                if k > 2:
                    pl.when(host)(lambda: advance_lent(k - 3, u))
                if k == 0:
                    @pl.when(u + 2 < UNITS)
                    def _():
                        load(u + 2).wait()
                        exchange(0, u + 2).start()

        for number, tasks in plan.items():
            @pl.when(step == number)
            def _():
                for task in tasks:
                    task()

    @pl.when(lender)
    def _():
        for k in range(3, FACTORS):
            own_copy(k).wait()

        @pl.loop(0, UNITS)
        def _(u):
            give_back(u).wait_recv()
            store(u).start()

    @pl.loop(0, UNITS)
    def _(u):
        store(u).wait()
        for k in range(3):
            exchange(k, u).wait_send()

        @pl.when(jnp.logical_not(host))
        def _():
            exchange(3, u).wait_send()

        @pl.when(jnp.logical_not(lender))
        def _():
            exchange(4, u).wait_send()

        @pl.when(host)
        def _():
            from_lent(u).wait_send()
            give_back(u).wait_send()

    def finish(k):
        if k < FACTORS:
            swap(k).wait_send()
        for half in range(2):
            fan_drain(k, half)

    for k in range(3):
        finish(k)
    on(keeper, (finish, 3), (finish, 4))()
    on(host, (finish, 5), (finish, 6))()

    @pl.when(lender)
    def _():
        for i in range(2):
            slab(i, col, 0).wait_send()
            slab(i, across, 1).wait_send()


def body(weight, blocks):
    f32 = jnp.float32
    dma = pltpu.SemaphoreType.DMA
    tiles = (UNITS, HALF, LANES)
    return pl.pallas_call(
        kernel,
        out_shape=jax.ShapeDtypeStruct(weight.shape, weight.dtype),
        in_specs=[pl.BlockSpec(memory_space=pl.ANY)] * 2,
        out_specs=pl.BlockSpec(memory_space=pl.ANY),
        scratch_shapes=[
            pltpu.VMEM((FACTORS,) + tiles, f32),
            pltpu.VMEM((FACTORS,) + tiles, f32),
            pltpu.VMEM(tiles, f32),
            pltpu.VMEM(tiles, f32),
            pltpu.VMEM(tiles, f32),
            pltpu.VMEM((SETS, 2, GROUP, HALF // GROUP, 2 * HALF), f32),
            pltpu.VMEM((SETS, 2, 2 * HALF, 2 * HALF), jnp.bfloat16),
            dma((UNITS,)),
            dma((UNITS,)),
            dma((FACTORS, UNITS)),
            dma((FACTORS, UNITS)),
            dma((UNITS,)),
            dma((UNITS,)),
            dma((UNITS,)),
            dma((UNITS,)),
            dma((2, 2)),
            dma((2, 2)),
            dma((FACTORS,)),
            dma((SETS, 2)),
            dma((SETS, 2, GROUP)),
            dma((FACTORS,)),
            dma((FACTORS,)),
        ],
        compiler_params=pltpu.CompilerParams(
            collective_id=0, has_side_effects=True, vmem_limit_bytes=60 * 1024 * 1024
        ),
    )(weight, blocks)


def solution(mesh):
    return jax.shard_map(
        body,
        mesh=mesh,
        in_specs=(P("row", "col"), P(None, ("row", "col"), None)),
        out_specs=P("row", "col"),
        check_vma=False,
    )
```

```python
import functools

import jax
import jax.numpy as jnp
from jax import lax
from jax.experimental import pallas as pl
from jax.experimental.pallas import tpu as pltpu
from jax.sharding import PartitionSpec as P

MESH = pl.DeviceIdType.MESH
FACTORS = 5
UNITS = 16
HALF = 256
LANES = 128
GROUP = 8
SETS = 7
LENT = ((5, 3), (6, 4))
FIRST = (0, 2, 6, 9, 12)
PERIOD = (2, 2, 2, 2, 2)
STEPS = FIRST[-1] + PERIOD[-1] * (UNITS - 1) + 1
SWAP_STEP = 7


def partner_of(index, stride):
    return index + stride - 2 * stride * lax.rem(index // stride, 2)


def remote(src, dst, send, recv, where):
    return pltpu.make_async_remote_copy(
        src_ref=src, dst_ref=dst, send_sem=send, recv_sem=recv, device_id=where, device_id_type=MESH
    )


def kernel(
    weight, blocks, out, w, r, done, w_lent, r_lent, raw, coef,
    load_sem, store_sem, send_sem, recv_sem, lent_send, lent_recv, back_send, back_recv, slab_send, slab_recv, own_sem, fan_send, fan_recv, swap_send, swap_recv,
):
    row, col = lax.axis_index("row"), lax.axis_index("col")
    z_hi, slot = col // GROUP, lax.rem(col, GROUP)
    y, core = slot // 2, lax.rem(slot, 2)
    turn = 1 - 2 * core
    front = lax.rem(y + 4 + turn, 4) * 2 + core
    back = lax.rem(y + 4 - turn, 4) * 2 + core
    far = lax.rem(y + 2, 4) * 2 + core
    twin = y * 2 + 1 - core
    own, other = z_hi, 1 - z_hi
    across = lax.rem(col + GROUP, 2 * GROUP)
    partners = [partner_of(row, 1 << k) for k in range(FACTORS)]
    x, z_lo = lax.rem(row, 4), row // 4
    lender = (z_lo == 1) | (z_lo == 6)
    host = (z_lo == 3) | (z_lo == 4)
    facing_lent = (z_lo == 2) | (z_lo == 5)
    pair = partners[3]
    lent_far = partner_of(pair, 16)
    far_host = partner_of(partners[4], 8)

    def half_of(u):
        return lax.rem(u // (UNITS // 2) + z_hi, 2)

    def tile(ref, u):
        rows = pl.ds(pl.multiple_of(half_of(u) * HALF, HALF), HALF)
        columns = pl.ds(pl.multiple_of(lax.rem(u, UNITS // 2) * LANES, LANES), LANES)
        return ref.at[rows, columns]

    def load(u):
        return pltpu.make_async_copy(tile(weight, u), w.at[0, u], load_sem.at[u])

    def store(u):
        return pltpu.make_async_copy(done.at[u], tile(out, u), store_sem.at[u])

    def exchange(k, u):
        return remote(w.at[k, u], r.at[k, u], send_sem.at[k, u], recv_sem.at[k, u], {"row": partners[k]})

    def to_lent(u):
        return remote(w.at[4, u], r_lent.at[u], send_sem.at[4, u], lent_recv.at[u], {"row": far_host})

    def from_lent(u):
        return remote(w_lent.at[u], r.at[4, u], lent_send.at[u], recv_sem.at[4, u], {"row": lent_far})

    def give_back(u):
        return remote(r_lent.at[u], done.at[u], back_send.at[u], back_recv.at[u], {"row": pair})

    def slab(i, column, which):
        k, source = LENT[i]
        return remote(
            blocks.at[source], raw.at[k, z_hi, slot], slab_send.at[i, which], slab_recv.at[i, z_hi],
            {"row": pair, "col": column},
        )

    def slab_wait(i, half):
        part = raw.at[LENT[i][0], half, slot]
        remote(part, part, slab_send.at[i, 0], slab_recv.at[i, half], {"row": pair, "col": across}).wait_recv()

    def own_copy(k):
        return pltpu.make_async_copy(blocks.at[k], raw.at[k, z_hi, slot], own_sem.at[k])

    def swap(k):
        return remote(blocks.at[k], raw.at[k, z_hi, slot], swap_send.at[k], swap_recv.at[k], {"col": across})

    def fan(k, half, source, to):
        return remote(
            raw.at[k, half, source], raw.at[k, half, source], fan_send.at[k, half], fan_recv.at[k, half, source],
            {"col": z_hi * GROUP + to},
        )

    def fan_start(k, half):
        for to in (front, back, twin):
            fan(k, half, slot, to).start()

    def fan_relay(k, half):
        fan(k, half, back, front).wait_recv()
        fan(k, half, back, front).start()
        fan(k, half, back, twin).start()

    def fan_rest(k, half):
        for source in (front, far):
            fan(k, half, source, twin).wait_recv()
            fan(k, half, source, twin).start()

    def fan_collect(k, half):
        for i in range(4):
            fan(k, half, 2 * i + 1 - core, twin).wait_recv()

    def fan_drain(k, half):
        part = raw.at[k, half, pl.ds(0, GROUP - 1)]
        remote(part, part, fan_send.at[k, half], fan_recv.at[k, half, 0], {"col": across}).wait_send()

    @pl.loop(0, UNITS)
    def _(u):
        load(u).start()

    for k in range(FACTORS):
        own_copy(k).start()

    barrier = pltpu.get_barrier_semaphore()

    def greet(where):
        pl.semaphore_signal(barrier, inc=1, device_id=where, device_id_type=MESH)

    for p in partners[:4]:
        greet({"row": p})
    for mate in (front, back, twin):
        greet({"col": z_hi * GROUP + mate})
    greet({"col": across})

    @pl.when(lender)
    def _():
        greet({"row": pair, "col": across})

    @pl.when(facing_lent)
    def _():
        greet({"row": far_host})

    @pl.when(host)
    def _():
        greet({"row": pair, "col": across})
        greet({"row": lent_far})

    @pl.when(jnp.logical_not(lender | facing_lent))
    def _():
        greet({"row": partners[4]})

    @pl.when(host)
    def _():
        pl.semaphore_wait(barrier, FACTORS + 4 + 2)

    @pl.when(jnp.logical_not(host))
    def _():
        pl.semaphore_wait(barrier, FACTORS + 4)

    for u in range(2):
        load(u).wait()
        exchange(0, u).start()

    @pl.when(lender)
    def _():
        for i in range(2):
            slab(i, col, 0).start()

    keeper = jnp.logical_not(lender)

    def on(condition, *tasks):
        def run():
            @pl.when(condition)
            def _():
                for f, *args in tasks:
                    f(*args)
        return run

    def always(*tasks):
        def run():
            for f, *args in tasks:
                f(*args)
        return run

    def first(k):
        own_copy(k).wait()
        fan_start(k, own)

    def take_swap(k):
        swap(k).wait_recv()
        fan_start(k, other)

    def take_slab(i, half):
        slab_wait(i, half)
        fan_start(LENT[i][0], half)

    for k in range(3):
        first(k)
    on(keeper, (first, 3), (first, 4))()
    for k in range(3):
        swap(k).start()
    on(keeper, (lambda: [swap(k).start() for k in (3, 4)],))()

    @pl.when(lender)
    def _():
        for i in range(2):
            slab(i, across, 1).start()

    for k in range(2):
        fan_relay(k, own)
    fan_rest(0, own)
    on(host, (take_slab, 0, own), (take_slab, 1, own))()

    plan = {}

    def at(step, task):
        plan.setdefault(step, []).append(task)

    at(0, always((fan_rest, 1, own), (fan_relay, 2, own)))
    at(1, always((fan_rest, 2, own)))
    at(1, on(keeper, (fan_relay, 3, own)))
    at(1, on(host, (fan_relay, 5, own)))
    at(2, on(keeper, (fan_rest, 3, own), (fan_relay, 4, own)))
    at(2, on(host, (fan_rest, 5, own), (fan_relay, 6, own)))
    at(3, on(keeper, (fan_rest, 4, own)))
    at(3, on(host, (fan_rest, 6, own)))
    for place, k in enumerate((0, 1, 2, 3, 5, 4, 6)):
        take = (take_swap, k) if k < FACTORS else (take_slab, k - FACTORS, other)
        who = always if k < 3 else functools.partial(on, keeper if k < FACTORS else host)
        at(SWAP_STEP + 2 * place, who(take))
        at(SWAP_STEP + 2 * place + 1, who((fan_relay, k, other)))
        at(SWAP_STEP + 2 * place + 2, who((fan_rest, k, other)))

    def prepare(k, half):
        fan_collect(k, half)
        block = raw[k, half].reshape(HALF, 2 * HALF)
        high = block.astype(jnp.bfloat16)
        coef[k, half, pl.ds(0, HALF), :] = high
        coef[k, half, pl.ds(HALF, HALF), :] = (block - high.astype(jnp.float32)).astype(jnp.bfloat16)

    def multiply(k, half, own, other):
        x = jnp.concatenate([own, other], axis=0)
        high = x.astype(jnp.bfloat16)
        low = (x - high.astype(jnp.float32)).astype(jnp.bfloat16)
        product = jnp.dot(
            coef[k, half], jnp.concatenate([high, low], axis=1), preferred_element_type=jnp.float32
        )
        cross = product[:HALF, LANES:] + product[HALF:, :LANES]
        return (product[:HALF, :LANES] + cross) + product[HALF:, LANES:]

    def advance(k, u):
        half = half_of(u)

        @pl.when(lax.rem(u, UNITS // 2) == 0)
        def _():
            prepare(k, half)

        exchange(k, u).wait_recv()
        y = multiply(k, half, w[k, u], r[k, u])
        if k + 1 == FACTORS:
            done[u] = y
            store(u).start()
        else:
            w[k + 1, u] = y
            if k < 2:
                exchange(k + 1, u).start()
            elif k == 2:
                pl.when(jnp.logical_not(host))(lambda: exchange(3, u).start())
            else:
                pl.when(facing_lent)(lambda: to_lent(u).start())
                pl.when(jnp.logical_not(facing_lent))(lambda: exchange(4, u).start())

    def advance_lent(i, u):
        half = half_of(u)
        k, source = LENT[i]

        @pl.when(lax.rem(u, UNITS // 2) == 0)
        def _():
            prepare(k, half)

        if i == 0:
            w_lent[u] = multiply(k, half, r[3, u], w[3, u])
            from_lent(u).start()
        else:
            to_lent(u).wait_recv()
            r_lent[u] = multiply(k, half, w_lent[u], r_lent[u])
            give_back(u).start()

    @pl.loop(0, STEPS)
    def _(step):
        for k in reversed(range(FACTORS)):
            since = step - FIRST[k]
            u = since // PERIOD[k]
            here = (since >= 0) & (lax.rem(since, PERIOD[k]) == 0) & (u < UNITS)
            if k > 2:
                here = here & keeper

            @pl.when(here)
            def _():
                advance(k, u)
                if k > 2:
                    pl.when(host)(lambda: advance_lent(k - 3, u))
                if k == 0:
                    @pl.when(u + 2 < UNITS)
                    def _():
                        load(u + 2).wait()
                        exchange(0, u + 2).start()

        for number, tasks in plan.items():
            @pl.when(step == number)
            def _():
                for task in tasks:
                    task()

    @pl.when(lender)
    def _():
        for k in range(3, FACTORS):
            own_copy(k).wait()

        @pl.loop(0, UNITS)
        def _(u):
            give_back(u).wait_recv()
            store(u).start()

    @pl.loop(0, UNITS)
    def _(u):
        store(u).wait()
        for k in range(3):
            exchange(k, u).wait_send()

        @pl.when(jnp.logical_not(host))
        def _():
            exchange(3, u).wait_send()

        @pl.when(jnp.logical_not(lender))
        def _():
            exchange(4, u).wait_send()

        @pl.when(host)
        def _():
            from_lent(u).wait_send()
            give_back(u).wait_send()

    def finish(k):
        if k < FACTORS:
            swap(k).wait_send()
        for half in range(2):
            fan_drain(k, half)

    for k in range(3):
        finish(k)
    on(keeper, (finish, 3), (finish, 4))()
    on(host, (finish, 5), (finish, 6))()

    @pl.when(lender)
    def _():
        for i in range(2):
            slab(i, col, 0).wait_send()
            slab(i, across, 1).wait_send()


def body(weight, blocks):
    f32 = jnp.float32
    dma = pltpu.SemaphoreType.DMA
    tiles = (UNITS, HALF, LANES)
    return pl.pallas_call(
        kernel,
        out_shape=jax.ShapeDtypeStruct(weight.shape, weight.dtype),
        in_specs=[pl.BlockSpec(memory_space=pl.ANY)] * 2,
        out_specs=pl.BlockSpec(memory_space=pl.ANY),
        scratch_shapes=[
            pltpu.VMEM((FACTORS,) + tiles, f32),
            pltpu.VMEM((FACTORS,) + tiles, f32),
            pltpu.VMEM(tiles, f32),
            pltpu.VMEM(tiles, f32),
            pltpu.VMEM(tiles, f32),
            pltpu.VMEM((SETS, 2, GROUP, HALF // GROUP, 2 * HALF), f32),
            pltpu.VMEM((SETS, 2, 2 * HALF, 2 * HALF), jnp.bfloat16),
            dma((UNITS,)),
            dma((UNITS,)),
            dma((FACTORS, UNITS)),
            dma((FACTORS, UNITS)),
            dma((UNITS,)),
            dma((UNITS,)),
            dma((UNITS,)),
            dma((UNITS,)),
            dma((2, 2)),
            dma((2, 2)),
            dma((FACTORS,)),
            dma((SETS, 2)),
            dma((SETS, 2, GROUP)),
            dma((FACTORS,)),
            dma((FACTORS,)),
        ],
        compiler_params=pltpu.CompilerParams(
            collective_id=0, has_side_effects=True, vmem_limit_bytes=60 * 1024 * 1024
        ),
    )(weight, blocks)


def solution(mesh):
    return jax.shard_map(
        body,
        mesh=mesh,
        in_specs=(P("row", "col"), P(None, ("row", "col"), None)),
        out_specs=P("row", "col"),
        check_vma=False,
    )
```

```python
import functools

import jax
import jax.numpy as jnp
from jax import lax
from jax.experimental import pallas as pl
from jax.experimental.pallas import tpu as pltpu
from jax.sharding import PartitionSpec as P

MESH = pl.DeviceIdType.MESH
FACTORS = 5
UNITS = 16
HALF = 256
LANES = 128
GROUP = 8
SETS = 7
LENT = ((5, 3), (6, 4))
FIRST = (0, 2, 6, 9, 12)
PERIOD = (2, 2, 2, 2, 2)
STEPS = FIRST[-1] + PERIOD[-1] * (UNITS - 1) + 1
SWAP_STEP = 7


def partner_of(index, stride):
    return index + stride - 2 * stride * lax.rem(index // stride, 2)


def remote(src, dst, send, recv, where):
    return pltpu.make_async_remote_copy(
        src_ref=src, dst_ref=dst, send_sem=send, recv_sem=recv, device_id=where, device_id_type=MESH
    )


def kernel(
    weight, blocks, out, w, r, done, w_lent, r_lent, raw, coef,
    load_sem, store_sem, send_sem, recv_sem, lent_send, lent_recv, back_send, back_recv, slab_send, slab_recv, own_sem, fan_send, fan_recv, swap_send, swap_recv,
):
    row, col = lax.axis_index("row"), lax.axis_index("col")
    z_hi, slot = col // GROUP, lax.rem(col, GROUP)
    y, core = slot // 2, lax.rem(slot, 2)
    turn = 1 - 2 * core
    front = lax.rem(y + 4 + turn, 4) * 2 + core
    back = lax.rem(y + 4 - turn, 4) * 2 + core
    far = lax.rem(y + 2, 4) * 2 + core
    twin = y * 2 + 1 - core
    own, other = z_hi, 1 - z_hi
    across = lax.rem(col + GROUP, 2 * GROUP)
    partners = [partner_of(row, 1 << k) for k in range(FACTORS)]
    x, z_lo = lax.rem(row, 4), row // 4
    lender = (z_lo == 1) | (z_lo == 6)
    host = (z_lo == 3) | (z_lo == 4)
    facing_lent = (z_lo == 2) | (z_lo == 5)
    pair = partners[3]
    lent_far = partner_of(pair, 16)
    far_host = partner_of(partners[4], 8)

    def half_of(u):
        return lax.rem(u // (UNITS // 2) + z_hi, 2)

    def tile(ref, u):
        rows = pl.ds(pl.multiple_of(half_of(u) * HALF, HALF), HALF)
        columns = pl.ds(pl.multiple_of(lax.rem(u, UNITS // 2) * LANES, LANES), LANES)
        return ref.at[rows, columns]

    def load(u):
        return pltpu.make_async_copy(tile(weight, u), w.at[0, u], load_sem.at[u])

    def store(u):
        return pltpu.make_async_copy(done.at[u], tile(out, u), store_sem.at[u])

    def exchange(k, u):
        return remote(w.at[k, u], r.at[k, u], send_sem.at[k, u], recv_sem.at[k, u], {"row": partners[k]})

    def to_lent(u):
        return remote(w.at[4, u], r_lent.at[u], send_sem.at[4, u], lent_recv.at[u], {"row": far_host})

    def from_lent(u):
        return remote(w_lent.at[u], r.at[4, u], lent_send.at[u], recv_sem.at[4, u], {"row": lent_far})

    def give_back(u):
        return remote(r_lent.at[u], done.at[u], back_send.at[u], back_recv.at[u], {"row": pair})

    def slab(i, column, which):
        k, source = LENT[i]
        return remote(
            blocks.at[source], raw.at[k, z_hi, slot], slab_send.at[i, which], slab_recv.at[i, z_hi],
            {"row": pair, "col": column},
        )

    def slab_wait(i, half):
        part = raw.at[LENT[i][0], half, slot]
        remote(part, part, slab_send.at[i, 0], slab_recv.at[i, half], {"row": pair, "col": across}).wait_recv()

    def own_copy(k):
        return pltpu.make_async_copy(blocks.at[k], raw.at[k, z_hi, slot], own_sem.at[k])

    def swap(k):
        return remote(blocks.at[k], raw.at[k, z_hi, slot], swap_send.at[k], swap_recv.at[k], {"col": across})

    def fan(k, half, source, to):
        return remote(
            raw.at[k, half, source], raw.at[k, half, source], fan_send.at[k, half], fan_recv.at[k, half, source],
            {"col": z_hi * GROUP + to},
        )

    def fan_start(k, half):
        for to in (front, back, twin):
            fan(k, half, slot, to).start()

    def fan_relay(k, half):
        fan(k, half, back, front).wait_recv()
        fan(k, half, back, front).start()
        fan(k, half, back, twin).start()

    def fan_rest(k, half):
        for source in (front, far):
            fan(k, half, source, twin).wait_recv()
            fan(k, half, source, twin).start()

    def fan_collect(k, half):
        for i in range(4):
            fan(k, half, 2 * i + 1 - core, twin).wait_recv()

    def fan_drain(k, half):
        part = raw.at[k, half, pl.ds(0, GROUP - 1)]
        remote(part, part, fan_send.at[k, half], fan_recv.at[k, half, 0], {"col": across}).wait_send()

    @pl.loop(0, UNITS)
    def _(u):
        load(u).start()

    for k in range(FACTORS):
        own_copy(k).start()

    barrier = pltpu.get_barrier_semaphore()

    def greet(where):
        pl.semaphore_signal(barrier, inc=1, device_id=where, device_id_type=MESH)

    for p in partners[:4]:
        greet({"row": p})
    for mate in (front, back, twin):
        greet({"col": z_hi * GROUP + mate})
    greet({"col": across})

    @pl.when(lender)
    def _():
        greet({"row": pair, "col": across})

    @pl.when(facing_lent)
    def _():
        greet({"row": far_host})

    @pl.when(host)
    def _():
        greet({"row": pair, "col": across})
        greet({"row": lent_far})

    @pl.when(jnp.logical_not(lender | facing_lent))
    def _():
        greet({"row": partners[4]})

    @pl.when(host)
    def _():
        pl.semaphore_wait(barrier, FACTORS + 4 + 2)

    @pl.when(jnp.logical_not(host))
    def _():
        pl.semaphore_wait(barrier, FACTORS + 4)

    for u in range(2):
        load(u).wait()
        exchange(0, u).start()

    @pl.when(lender)
    def _():
        for i in range(2):
            slab(i, col, 0).start()

    keeper = jnp.logical_not(lender)

    def on(condition, *tasks):
        def run():
            @pl.when(condition)
            def _():
                for f, *args in tasks:
                    f(*args)
        return run

    def always(*tasks):
        def run():
            for f, *args in tasks:
                f(*args)
        return run

    def first(k):
        own_copy(k).wait()
        fan_start(k, own)

    def take_swap(k):
        swap(k).wait_recv()
        fan_start(k, other)

    def take_slab(i, half):
        slab_wait(i, half)
        fan_start(LENT[i][0], half)

    for k in range(3):
        first(k)
    on(keeper, (first, 3), (first, 4))()
    for k in range(3):
        swap(k).start()

    @pl.when(lender)
    def _():
        for i in range(2):
            slab(i, across, 1).start()

    for k in range(2):
        fan_relay(k, own)
    fan_rest(0, own)
    on(host, (take_slab, 0, own), (take_slab, 1, own))()

    plan = {}

    def at(step, task):
        plan.setdefault(step, []).append(task)

    at(0, always((fan_rest, 1, own), (fan_relay, 2, own)))
    at(1, always((fan_rest, 2, own)))
    at(1, on(keeper, (fan_relay, 3, own)))
    at(1, on(host, (fan_relay, 5, own)))
    at(2, on(keeper, (fan_rest, 3, own), (fan_relay, 4, own)))
    at(2, on(host, (fan_rest, 5, own), (fan_relay, 6, own)))
    at(3, on(keeper, (fan_rest, 4, own)))
    at(3, on(host, (fan_rest, 6, own)))
    at(2, on(keeper, (lambda: swap(3).start(),)))
    at(4, on(keeper, (lambda: swap(4).start(),)))
    for place, k in enumerate((0, 1, 2, 3, 5, 4, 6)):
        take = (take_swap, k) if k < FACTORS else (take_slab, k - FACTORS, other)
        who = always if k < 3 else functools.partial(on, keeper if k < FACTORS else host)
        at(SWAP_STEP + 2 * place, who(take))
        at(SWAP_STEP + 2 * place + 1, who((fan_relay, k, other)))
        at(SWAP_STEP + 2 * place + 2, who((fan_rest, k, other)))

    def prepare(k, half):
        fan_collect(k, half)
        block = raw[k, half].reshape(HALF, 2 * HALF)
        high = block.astype(jnp.bfloat16)
        coef[k, half, pl.ds(0, HALF), :] = high
        coef[k, half, pl.ds(HALF, HALF), :] = (block - high.astype(jnp.float32)).astype(jnp.bfloat16)

    def multiply(k, half, own, other):
        x = jnp.concatenate([own, other], axis=0)
        high = x.astype(jnp.bfloat16)
        low = (x - high.astype(jnp.float32)).astype(jnp.bfloat16)
        product = jnp.dot(
            coef[k, half], jnp.concatenate([high, low], axis=1), preferred_element_type=jnp.float32
        )
        cross = product[:HALF, LANES:] + product[HALF:, :LANES]
        return (product[:HALF, :LANES] + cross) + product[HALF:, LANES:]

    def advance(k, u):
        half = half_of(u)

        @pl.when(lax.rem(u, UNITS // 2) == 0)
        def _():
            prepare(k, half)

        exchange(k, u).wait_recv()
        y = multiply(k, half, w[k, u], r[k, u])
        if k + 1 == FACTORS:
            done[u] = y
            store(u).start()
        else:
            w[k + 1, u] = y
            if k < 2:
                exchange(k + 1, u).start()
            elif k == 2:
                pl.when(jnp.logical_not(host))(lambda: exchange(3, u).start())
            else:
                pl.when(facing_lent)(lambda: to_lent(u).start())
                pl.when(jnp.logical_not(facing_lent))(lambda: exchange(4, u).start())

    def advance_lent(i, u):
        half = half_of(u)
        k, source = LENT[i]

        @pl.when(lax.rem(u, UNITS // 2) == 0)
        def _():
            prepare(k, half)

        if i == 0:
            w_lent[u] = multiply(k, half, r[3, u], w[3, u])
            from_lent(u).start()
        else:
            to_lent(u).wait_recv()
            r_lent[u] = multiply(k, half, w_lent[u], r_lent[u])
            give_back(u).start()

    @pl.loop(0, STEPS)
    def _(step):
        for k in reversed(range(FACTORS)):
            since = step - FIRST[k]
            u = since // PERIOD[k]
            here = (since >= 0) & (lax.rem(since, PERIOD[k]) == 0) & (u < UNITS)
            if k > 2:
                here = here & keeper

            @pl.when(here)
            def _():
                advance(k, u)
                if k > 2:
                    pl.when(host)(lambda: advance_lent(k - 3, u))
                if k == 0:
                    @pl.when(u + 2 < UNITS)
                    def _():
                        load(u + 2).wait()
                        exchange(0, u + 2).start()

        for number, tasks in plan.items():
            @pl.when(step == number)
            def _():
                for task in tasks:
                    task()

    @pl.when(lender)
    def _():
        for k in range(3, FACTORS):
            own_copy(k).wait()

        @pl.loop(0, UNITS)
        def _(u):
            give_back(u).wait_recv()
            store(u).start()

    @pl.loop(0, UNITS)
    def _(u):
        store(u).wait()
        for k in range(3):
            exchange(k, u).wait_send()

        @pl.when(jnp.logical_not(host))
        def _():
            exchange(3, u).wait_send()

        @pl.when(jnp.logical_not(lender))
        def _():
            exchange(4, u).wait_send()

        @pl.when(host)
        def _():
            from_lent(u).wait_send()
            give_back(u).wait_send()

    def finish(k):
        if k < FACTORS:
            swap(k).wait_send()
        for half in range(2):
            fan_drain(k, half)

    for k in range(3):
        finish(k)
    on(keeper, (finish, 3), (finish, 4))()
    on(host, (finish, 5), (finish, 6))()

    @pl.when(lender)
    def _():
        for i in range(2):
            slab(i, col, 0).wait_send()
            slab(i, across, 1).wait_send()


def body(weight, blocks):
    f32 = jnp.float32
    dma = pltpu.SemaphoreType.DMA
    tiles = (UNITS, HALF, LANES)
    return pl.pallas_call(
        kernel,
        out_shape=jax.ShapeDtypeStruct(weight.shape, weight.dtype),
        in_specs=[pl.BlockSpec(memory_space=pl.ANY)] * 2,
        out_specs=pl.BlockSpec(memory_space=pl.ANY),
        scratch_shapes=[
            pltpu.VMEM((FACTORS,) + tiles, f32),
            pltpu.VMEM((FACTORS,) + tiles, f32),
            pltpu.VMEM(tiles, f32),
            pltpu.VMEM(tiles, f32),
            pltpu.VMEM(tiles, f32),
            pltpu.VMEM((SETS, 2, GROUP, HALF // GROUP, 2 * HALF), f32),
            pltpu.VMEM((SETS, 2, 2 * HALF, 2 * HALF), jnp.bfloat16),
            dma((UNITS,)),
            dma((UNITS,)),
            dma((FACTORS, UNITS)),
            dma((FACTORS, UNITS)),
            dma((UNITS,)),
            dma((UNITS,)),
            dma((UNITS,)),
            dma((UNITS,)),
            dma((2, 2)),
            dma((2, 2)),
            dma((FACTORS,)),
            dma((SETS, 2)),
            dma((SETS, 2, GROUP)),
            dma((FACTORS,)),
            dma((FACTORS,)),
        ],
        compiler_params=pltpu.CompilerParams(
            collective_id=0, has_side_effects=True, vmem_limit_bytes=60 * 1024 * 1024
        ),
    )(weight, blocks)


def solution(mesh):
    return jax.shard_map(
        body,
        mesh=mesh,
        in_specs=(P("row", "col"), P(None, ("row", "col"), None)),
        out_specs=P("row", "col"),
        check_vma=False,
    )
```
